32 devices in a mesh: dp: 32 (over z, y, x, core).
Axes of the slice: x: 2, y: 2, z: 4, core: 2. Of those that a mesh axis runs over, the one named last changes fastest.
Arguments:
- tokens: bfloat16 [8192, 1536], P('dp'), may hold values from -6 to 6
- cotangent: bfloat16 [8192, 1536], P('dp'), may hold values from -6 to 6
- lengths: int32 [256], P('dp'), may hold values from 0 to 256, as said below
- norm_gain: float32 [1536], replicated, may hold values from 0.5 to 1.5
- in_weight: bfloat16 [1536, 6448], replicated, may hold values from -0.15625 to 0.15625
- conv_weight: float32 [4, 3328], replicated, may hold values from -3 to 3
- conv_bias: float32 [3328], replicated, may hold values from -3 to 3
- dt_bias: float32 [48], replicated, may hold values from -6.9 to -2.3
- a_log: float32 [48], replicated, may hold values from 0 to 2.77
- skip_d: float32 [48], replicated, may hold values from 0.5 to 1.5
- gate_gain: float32 [3072], replicated, may hold values from 0.5 to 1.5
- out_weight: bfloat16 [3072, 1536], replicated, may hold values from -0.109375 to 0.109375
Outputs:
- output: float32 [8192, 1536], P('dp')
- grad_tokens: float32 [8192, 1536], P('dp')
- grad_in_weight: float32 [1536, 6448], P('dp')
- grad_out_weight: float32 [3072, 1536], P('dp')
- grad_norm_gain: float32 [1536], replicated
- grad_conv_weight: float32 [4, 3328], replicated
- grad_conv_bias: float32 [3328], replicated
- grad_dt_bias: float32 [48], replicated
- grad_a_log: float32 [48], replicated
- grad_skip: float32 [48], replicated
- grad_gate_gain: float32 [3072], replicated
The draws below stay inside these ranges and needn't reach their ends.
Inputs may be any that keep to these rules, and one draw needn't show every extreme that they name: Each device's 8 entries are the lengths of its packed sequences from its first row on, zero for empty slots; they sum to at most 256, and the rows after them are padding. Some device holds one sequence of 256 rows.
All inputs are finite; a program needn't handle non-finite values.
Results may differ from the reference program's by a relative error of at most 0.0065.
Values sent between devices are 32-bit elements; how exact they have to be, the bound alone decides.
No kernel may reach another device: no remote copies, remote signals or barrier semaphores. Data moves between devices by JAX's collectives and lax.ppermute only.
A program may use at most 256 MiB of HBM per device.

```python
import jax
import jax.numpy as jnp
from jax import lax

D = 1536
INNER = 3072
HEADS = 48
CONV = 4
SPAN = 256
TOK_DEV = 256
SEQ_DEV = 8
TOKENS = 8192
SEQS = 256
PROJ = 6448
CDIM = 3328
N_DP = 32


def draw_lengths(key, part):
    device_count = SEQS // SEQ_DEV
    first_key, second_key, third_key, fourth_key = jax.random.split(jax.random.fold_in(key, 17), 4)
    first_draw = jax.random.randint(first_key, (device_count,), 0, TOK_DEV + 1)
    second_draw = jax.random.randint(second_key, (device_count,), 0, TOK_DEV + 1)
    product_share = first_draw * second_draw // TOK_DEV
    live_counts = TOK_DEV // 16 + product_share * 15 // 16
    full_device = jax.random.randint(third_key, (), 0, device_count)
    is_full = jnp.arange(device_count) == full_device
    live_counts = jnp.where(is_full, TOK_DEV, live_counts)
    raw_cuts = jax.random.randint(fourth_key, (device_count, SEQ_DEV - 1), 0, 65537)
    cut_points = jnp.sort(raw_cuts * live_counts[:, None] // 65536, axis=1)
    cut_points = jnp.where(is_full[:, None], live_counts[:, None], cut_points)
    boundaries = jnp.concatenate([jnp.zeros((device_count, 1), jnp.int32), cut_points.astype(jnp.int32), live_counts[:, None].astype(jnp.int32)], axis=1)
    seq_lengths = boundaries[:, 1:] - boundaries[:, :-1]
    return seq_lengths.reshape(SEQS).astype(jnp.int32)


def levels(rng, dims, shards, least, top_value):
    factor_of, own = 1.0, jax.random.fold_in(rng, 6)
    for dim, shards_of in shards:
        heights = jnp.exp(jax.random.uniform(jax.random.fold_in(own, dim), (shards_of,), jnp.float32, least / len(shards), top_value / len(shards)))
        factor_of = factor_of * jnp.repeat(heights, dims[dim] // shards_of).reshape([-1 if axis == dim else 1 for axis in range(len(dims))])
    return factor_of


def normal_values(stream_key, extent, deviation, most, cuts=(), held_as=jnp.bfloat16):
    entries = deviation * jax.random.normal(stream_key, extent, jnp.float32)
    if cuts:
        entries = entries * levels(stream_key, extent, cuts, -0.22, 0.18)
    return jnp.clip(entries, -most, most).astype(held_as)


def setup_inputs(seed: int = 0) -> dict:
    splits = jax.random.split(jax.random.key(seed), 13)
    tokens = normal_values(splits[0], (TOKENS, D), 1.0, 6.0, ((0, 32),))
    cotangent = normal_values(splits[1], (TOKENS, D), 1.0, 6.0, ((0, 32),))
    lengths = draw_lengths(jax.random.fold_in(splits[12], 71), 0)
    norm_gain = jnp.clip(1.0 + 0.1 * jax.random.normal(splits[3], (D,), jnp.float32), 0.5, 1.5)
    in_weight = normal_values(splits[4], (D, PROJ), D ** -0.5, 0.15625)
    conv_weight = normal_values(splits[5], (CONV, CDIM), CONV ** -0.5, 3.0, (), jnp.float32)
    conv_bias = normal_values(splits[6], (CDIM,), 0.5, 3.0, (), jnp.float32)
    dt_bias = jnp.clip(jax.random.uniform(splits[7], (HEADS,), jnp.float32, -6.9, -2.3), -6.9, -2.3)
    a_log = jnp.clip(jax.random.uniform(splits[8], (HEADS,), jnp.float32, 0.0, 2.77), 0.0, 2.77)
    skip_d = jnp.clip(jax.random.uniform(splits[9], (HEADS,), jnp.float32, 0.5, 1.5), 0.5, 1.5)
    gate_gain = jnp.clip(1.0 + 0.1 * jax.random.normal(splits[10], (INNER,), jnp.float32), 0.5, 1.5)
    out_weight = normal_values(splits[11], (INNER, D), INNER ** -0.5, 0.109375)
    return {"tokens": tokens, "cotangent": cotangent, "lengths": lengths, "norm_gain": norm_gain, "in_weight": in_weight, "conv_weight": conv_weight, "conv_bias": conv_bias, "dt_bias": dt_bias, "a_log": a_log, "skip_d": skip_d, "gate_gain": gate_gain, "out_weight": out_weight}


epsilon = 1e-05
masked_log = -10000.0
highest = lax.Precision.HIGHEST

def norm_rows(float_rows, gain_vector):
    scale_rows = lax.rsqrt(lax.optimization_barrier(jnp.mean(float_rows * float_rows, axis=-1, keepdims=True)) + epsilon)
    return float_rows * scale_rows * gain_vector

def segment_rows(seq_lengths, count_rows):
    seq_ends = jnp.cumsum(seq_lengths).astype(jnp.int32)
    positions = jnp.arange(count_rows, dtype=jnp.int32)
    segment_ids = lax.optimization_barrier(jnp.sum((positions[:, None] >= seq_ends[None, :]).astype(jnp.int32), axis=1)).astype(jnp.int32)
    live_rows = (segment_ids < seq_lengths.shape[0]).astype(jnp.float32)
    return (segment_ids, live_rows)

def block_step(carry_in, pieces):
    carry_state, prior_segment = carry_in
    value_block, input_block, output_block, step_block, log_block, segment_block = pieces
    cumulative = jnp.cumsum(log_block, axis=0)
    index_rows = jnp.arange(segment_block.shape[0])
    allowed = (segment_block[:, None] == segment_block[None, :]) & (index_rows[:, None] >= index_rows[None, :])
    heads_first = cumulative.T
    spread = heads_first[:, :, None] - heads_first[:, None, :]
    decays = jnp.exp(jnp.where(allowed[None], spread, masked_log))
    inner_products = jnp.dot(output_block, input_block.T, precision=highest)
    mixing = decays * inner_products[None] * step_block.T[:, None, :]
    result = jnp.einsum('hts,shp->thp', mixing, value_block, precision=highest)
    carried = (segment_block == prior_segment).astype(jnp.float32)
    from_state = jnp.einsum('tn,hpn->thp', output_block, carry_state, precision=highest)
    result = result + jnp.exp(cumulative)[:, :, None] * carried[:, None, None] * from_state
    last_segment = segment_block[-1]
    kept_rows = (segment_block == last_segment).astype(jnp.float32)
    toward_end = jnp.exp(cumulative[-1][None, :] - cumulative) * step_block * kept_rows[:, None]
    fresh_state = jnp.einsum('shp,sn->hpn', value_block * toward_end[:, :, None], input_block, precision=highest)
    continues = (prior_segment == last_segment).astype(jnp.float32)
    new_state = jnp.exp(cumulative[-1])[:, None, None] * carry_state * continues + fresh_state
    return ((new_state, last_segment), result)

def state_space(values, input_map, output_map, step_sizes, log_decay, segment_ids):
    count_rows, head_count, head_width = values.shape
    state_dim = input_map.shape[1]
    blocks = count_rows // SPAN
    pieces = (values.reshape(blocks, SPAN, head_count, head_width), input_map.reshape(blocks, SPAN, state_dim), output_map.reshape(blocks, SPAN, state_dim), step_sizes.reshape(blocks, SPAN, head_count), log_decay.reshape(blocks, SPAN, head_count), segment_ids.reshape(blocks, SPAN))
    start_state = jnp.zeros((head_count, head_width, state_dim), jnp.float32)
    start_carry = (start_state, jnp.array(-1, jnp.int32))
    final_carry, results = lax.scan(jax.checkpoint(block_step), start_carry, pieces)
    return results.reshape(count_rows, head_count, head_width)

def mixer_branch(projected, segment_ids, conv_weight, conv_bias, dt_bias, a_log, skip_d, gate_gain):
    inner_width = gate_gain.shape[0]
    head_count = a_log.shape[0]
    channels = conv_bias.shape[0]
    state_dim = (channels - inner_width) // 2
    conv_taps = conv_weight.shape[0]
    count_rows = projected.shape[0]
    gate_part = projected[:, :inner_width]
    conv_in = projected[:, inner_width:inner_width + channels]
    step_raw = projected[:, inner_width + channels:]
    padded = jnp.concatenate([jnp.zeros((conv_taps - 1, channels), jnp.float32), conv_in], axis=0)
    padded_ids = jnp.concatenate([jnp.full((conv_taps - 1,), -1, jnp.int32), segment_ids], axis=0)
    summed = jnp.broadcast_to(conv_bias, conv_in.shape)
    for offset in range(conv_taps):
        matching = (padded_ids[offset:offset + count_rows] == segment_ids).astype(jnp.float32)
        summed = summed + conv_weight[offset] * padded[offset:offset + count_rows] * matching[:, None]
    activated = jax.nn.silu(summed)
    values = activated[:, :inner_width].reshape(count_rows, head_count, inner_width // head_count)
    input_map = activated[:, inner_width:inner_width + state_dim]
    output_map = activated[:, inner_width + state_dim:]
    step_sizes = jax.nn.softplus(step_raw + dt_bias)
    log_decay = -step_sizes * jnp.exp(a_log)
    mixed_out = state_space(values, input_map, output_map, step_sizes, log_decay, segment_ids)
    mixed_out = mixed_out + skip_d[None, :, None] * values
    gated_rows = mixed_out.reshape(count_rows, inner_width) * jax.nn.silu(gate_part)
    return norm_rows(gated_rows, gate_gain)

def layer_block(tokens, cotangent, seq_lengths, norm_gain, in_weight, conv_weight, conv_bias, dt_bias, a_log, skip_d, gate_gain, out_weight):
    count_rows = tokens.shape[0]
    segment_ids, live_rows = segment_rows(seq_lengths, count_rows)
    float_rows = tokens.astype(jnp.float32)
    normed = norm_rows(float_rows, norm_gain).astype(jnp.bfloat16)
    projected = jnp.dot(normed, in_weight, preferred_element_type=jnp.float32)
    small_params = (conv_weight, conv_bias, dt_bias, a_log, skip_d, gate_gain)

    def local_mixer(proj_rows, params):
        return mixer_branch(proj_rows, segment_ids, params[0], params[1], params[2], params[3], params[4], params[5])
    mixer_out, mixer_back = jax.vjp(local_mixer, projected, small_params)
    mixer_bf = mixer_out.astype(jnp.bfloat16)
    branch = jnp.dot(mixer_bf, out_weight, preferred_element_type=jnp.float32)
    output_rows = (float_rows + branch) * live_rows[:, None]
    upstream = cotangent * live_rows[:, None].astype(jnp.bfloat16)
    grad_out = lax.dot_general(mixer_bf, upstream, (((0,), (0,)), ((), ())), preferred_element_type=jnp.float32)
    grad_mixer = lax.dot_general(upstream, out_weight, (((1,), (1,)), ((), ())), preferred_element_type=jnp.float32)
    grad_proj, grad_small = mixer_back(grad_mixer)
    grad_proj_bf = grad_proj.astype(jnp.bfloat16)
    grad_in = lax.dot_general(normed, grad_proj_bf, (((0,), (0,)), ((), ())), preferred_element_type=jnp.float32)
    grad_normed = lax.dot_general(grad_proj_bf, in_weight, (((1,), (1,)), ((), ())), preferred_element_type=jnp.float32)
    norm_value, norm_back = jax.vjp(norm_rows, float_rows, norm_gain)
    grad_rows, grad_gain = norm_back(grad_normed)
    grad_tokens = upstream.astype(jnp.float32) + grad_rows
    return (output_rows, grad_tokens, grad_in, grad_out, grad_gain, grad_small)

def add_pair(first, second):
    return first + second

def reference(tokens, cotangent, lengths, norm_gain, in_weight, conv_weight, conv_bias, dt_bias, a_log, skip_d, gate_gain, out_weight):
    small_zero = (jnp.zeros(conv_weight.shape, jnp.float32), jnp.zeros(conv_bias.shape, jnp.float32), jnp.zeros(dt_bias.shape, jnp.float32), jnp.zeros(a_log.shape, jnp.float32), jnp.zeros(skip_d.shape, jnp.float32), jnp.zeros(gate_gain.shape, jnp.float32))
    start_totals = (jnp.zeros(in_weight.shape, jnp.float32), jnp.zeros(out_weight.shape, jnp.float32), jnp.zeros(norm_gain.shape, jnp.float32), small_zero)

    def visit(totals, pieces):
        token_piece, cot_piece, length_piece = pieces
        rows_out, rows_grad, grad_in, grad_out, grad_gain, grad_small = layer_block(token_piece, cot_piece, length_piece, norm_gain, in_weight, conv_weight, conv_bias, dt_bias, a_log, skip_d, gate_gain, out_weight)
        updated = (totals[0] + grad_in, totals[1] + grad_out, totals[2] + grad_gain, jax.tree.map(add_pair, totals[3], grad_small))
        return (updated, (rows_out, rows_grad))
    pieces = (tokens.reshape(N_DP, TOK_DEV, D), cotangent.reshape(N_DP, TOK_DEV, D), lengths.reshape(N_DP, SEQ_DEV))
    totals, stacked = lax.scan(visit, start_totals, pieces)
    small_sums = totals[3]
    return (stacked[0].reshape(TOKENS, D), stacked[1].reshape(TOKENS, D), totals[0], totals[1], totals[2], small_sums[0], small_sums[1], small_sums[2], small_sums[3], small_sums[4], small_sums[5])
```

```python
import functools

import jax
import jax.numpy as jnp
from jax import lax
from jax.experimental import pallas as pl
from jax.experimental.pallas import tpu as pltpu
from jax.sharding import PartitionSpec as P

SPAN = 256


epsilon = 1e-05
masked_log = -10000.0
highest = lax.Precision.HIGHEST


def norm_rows(float_rows, gain_vector):
    scale_rows = lax.rsqrt(jnp.mean(float_rows * float_rows, axis=-1, keepdims=True) + epsilon)
    return float_rows * scale_rows * gain_vector


def segment_rows(seq_lengths, count_rows):
    seq_ends = jnp.cumsum(seq_lengths)
    positions = jnp.arange(count_rows, dtype=jnp.int32)
    segment_ids = jnp.sum((positions[:, None] >= seq_ends[None, :]).astype(jnp.int32), axis=1)
    live_rows = (segment_ids < seq_lengths.shape[0]).astype(jnp.float32)
    return (segment_ids, live_rows)


def block_step(carry_in, pieces):
    carry_state, prior_segment = carry_in
    value_block, input_block, output_block, step_block, log_block, segment_block = pieces
    cumulative = jnp.cumsum(log_block, axis=0)
    index_rows = jnp.arange(segment_block.shape[0])
    allowed = (segment_block[:, None] == segment_block[None, :]) & (
        index_rows[:, None] >= index_rows[None, :]
    )
    heads_first = cumulative.T
    spread = heads_first[:, :, None] - heads_first[:, None, :]
    decays = jnp.exp(jnp.where(allowed[None], spread, masked_log))
    inner_products = jnp.dot(output_block, input_block.T, precision=highest)
    mixing = decays * inner_products[None] * step_block.T[:, None, :]
    result = jnp.einsum("hts,shp->thp", mixing, value_block, precision=highest)
    carried = (segment_block == prior_segment).astype(jnp.float32)
    from_state = jnp.einsum("tn,hpn->thp", output_block, carry_state, precision=highest)
    result = result + jnp.exp(cumulative)[:, :, None] * carried[:, None, None] * from_state
    last_segment = segment_block[-1]
    kept_rows = (segment_block == last_segment).astype(jnp.float32)
    toward_end = jnp.exp(cumulative[-1][None, :] - cumulative) * step_block * kept_rows[:, None]
    fresh_state = jnp.einsum(
        "shp,sn->hpn", value_block * toward_end[:, :, None], input_block, precision=highest
    )
    continues = (prior_segment == last_segment).astype(jnp.float32)
    new_state = jnp.exp(cumulative[-1])[:, None, None] * carry_state * continues + fresh_state
    return ((new_state, last_segment), result)


def state_space(values, input_map, output_map, step_sizes, log_decay, segment_ids):
    count_rows, head_count, head_width = values.shape
    state_dim = input_map.shape[1]
    blocks = count_rows // SPAN
    pieces = (
        values.reshape(blocks, SPAN, head_count, head_width),
        input_map.reshape(blocks, SPAN, state_dim),
        output_map.reshape(blocks, SPAN, state_dim),
        step_sizes.reshape(blocks, SPAN, head_count),
        log_decay.reshape(blocks, SPAN, head_count),
        segment_ids.reshape(blocks, SPAN),
    )
    start_state = jnp.zeros((head_count, head_width, state_dim), jnp.float32)
    start_carry = (start_state, jnp.array(-1, jnp.int32))
    final_carry, results = lax.scan(jax.checkpoint(block_step), start_carry, pieces)
    return results.reshape(count_rows, head_count, head_width)


def mixer_branch(projected, segment_ids, conv_weight, conv_bias, dt_bias, a_log, skip_d, gate_gain):
    inner_width = gate_gain.shape[0]
    head_count = a_log.shape[0]
    channels = conv_bias.shape[0]
    state_dim = (channels - inner_width) // 2
    conv_taps = conv_weight.shape[0]
    count_rows = projected.shape[0]
    gate_part = projected[:, :inner_width]
    conv_in = projected[:, inner_width : inner_width + channels]
    step_raw = projected[:, inner_width + channels :]
    padded = jnp.concatenate([jnp.zeros((conv_taps - 1, channels), jnp.float32), conv_in], axis=0)
    padded_ids = jnp.concatenate([jnp.full((conv_taps - 1,), -1, jnp.int32), segment_ids], axis=0)
    summed = jnp.broadcast_to(conv_bias, conv_in.shape)
    for offset in range(conv_taps):
        matching = (padded_ids[offset : offset + count_rows] == segment_ids).astype(jnp.float32)
        summed = (
            summed + conv_weight[offset] * padded[offset : offset + count_rows] * matching[:, None]
        )
    activated = jax.nn.silu(summed)
    values = activated[:, :inner_width].reshape(count_rows, head_count, inner_width // head_count)
    input_map = activated[:, inner_width : inner_width + state_dim]
    output_map = activated[:, inner_width + state_dim :]
    step_sizes = jax.nn.softplus(step_raw + dt_bias)
    log_decay = -step_sizes * jnp.exp(a_log)
    mixed_out = state_space(values, input_map, output_map, step_sizes, log_decay, segment_ids)
    mixed_out = mixed_out + skip_d[None, :, None] * values
    gated_rows = mixed_out.reshape(count_rows, inner_width) * jax.nn.silu(gate_part)
    return norm_rows(gated_rows, gate_gain)


GROUP = 8


def flip(array, bits):
    count = lax.axis_size("dp")
    return lax.ppermute(array, "dp", [(i, i ^ bits) for i in range(count)])


def pick(array, index, axis=0):
    return lax.dynamic_index_in_dim(array, index, axis, keepdims=False)


def product_kernel(lefts, rights, *refs):
    left_refs, right_refs = refs[:lefts], refs[lefts : lefts + rights]
    out_ref, right_held = refs[lefts + rights :]

    @pl.when(pl.program_id(0) == 0)
    def _():
        start = 0
        for ref in right_refs:
            right_held[start : start + ref.shape[0], :] = ref[...].astype(jnp.bfloat16)
            start += ref.shape[0]

    left = jnp.concatenate([ref[...].astype(jnp.bfloat16) for ref in left_refs], axis=1)
    out_ref[...] = jnp.dot(left, right_held[...], preferred_element_type=jnp.float32)


def factor_product(lefts, rights, block=128):
    rows = lefts[0].shape[0]
    depth = sum(left.shape[1] for left in lefts)
    columns = rights[0].shape[1]
    return pl.pallas_call(
        functools.partial(product_kernel, len(lefts), len(rights)),
        out_shape=jax.ShapeDtypeStruct((rows, columns), jnp.float32),
        grid=(rows // block,),
        in_specs=[pl.BlockSpec((block, left.shape[1]), lambda i: (i, 0)) for left in lefts]
        + [pl.BlockSpec(right.shape, lambda i: (0, 0)) for right in rights],
        out_specs=pl.BlockSpec((block, columns), lambda i: (i, 0)),
        scratch_shapes=[pltpu.VMEM((depth, columns), jnp.bfloat16)],
        cost_estimate=pl.CostEstimate(
            flops=2 * rows * depth * columns,
            bytes_accessed=4 * (rows * depth + depth * columns + rows * columns),
            transcendentals=0,
        ),
    )(*lefts, *rights)


def sum_all(arrays):
    flat = jnp.concatenate([array.reshape(-1) for array in arrays])
    total = flat.shape[0]
    flat = jnp.pad(flat, (0, -total % 1024))
    bits = 1
    while bits < lax.axis_size("dp"):
        flat = flat + flip(flat, bits)
        bits *= 2
    sums, start = [], 0
    for array in arrays:
        sums.append(flat[start : start + array.size].reshape(array.shape))
        start += array.size
    return sums


def line_scatter(parts):
    slabs = parts.shape[0]
    count = lax.axis_size("dp")
    slab = lax.axis_index("dp") // GROUP
    up_carry, down_carry = parts[slabs - 1], parts[0]
    for step in range(1, slabs):
        up_pairs = [(i, i + GROUP) for i in range(count - GROUP) if i // GROUP < step]
        down_pairs = [
            (i, i - GROUP) for i in range(GROUP, count) if slabs - 1 - i // GROUP < step
        ]
        up = lax.ppermute(up_carry, "dp", up_pairs)
        down = lax.ppermute(down_carry, "dp", down_pairs)
        if step < slabs - 1:
            up_carry = up + pick(parts, jnp.minimum(slabs - step + slab - 1, slabs - 1))
            down_carry = down + pick(parts, jnp.maximum(step - slabs + slab + 1, 0))
    return pick(parts, slab) + up + down


def sum_in_weight(normed, grad_proj):
    count = lax.axis_size("dp")
    place = lax.axis_index("dp")
    core, quarter = place % 2, place // 2 % 4
    slabs = count // GROUP
    tokens, width = normed.shape
    rows = width // count
    left = normed.T.astype(jnp.float32).reshape(slabs * 4, 2, rows, tokens)
    mine = pick(left, core, 1)
    left = jnp.concatenate([mine, flip(pick(left, 1 - core, 1), 1)], axis=-1)
    left = left.reshape(width // 2, 2 * tokens)
    left_x = flip(left, 2)
    lefts = (left, left_x, flip(left, 4), flip(left_x, 4))
    columns = grad_proj.shape[1]
    padded = -(-columns // 512) * 512
    right = jnp.pad(grad_proj.astype(jnp.float32), ((0, 0), (0, padded - columns)))
    right = right.reshape(tokens, 4, padded // 4)
    rights = []
    for offset in range(4):
        piece = pick(right, quarter ^ offset, 1)
        if offset:
            piece = flip(piece, 2 * offset)
        rights += [piece, flip(piece, 1)]
    product = factor_product(lefts, rights)
    share = line_scatter(product.reshape(slabs, 4, rows, padded // 4))
    final = jnp.zeros((4, rows, padded // 4), jnp.float32)
    for offset in range(4):
        piece = pick(share, quarter ^ offset)
        if offset:
            piece = flip(piece, 2 * offset)
        final = lax.dynamic_update_index_in_dim(final, piece, quarter ^ offset, 0)
    return final.transpose(1, 0, 2).reshape(rows, padded)[:, :columns]


def sum_out_weight(mixer, upstream):
    count = lax.axis_size("dp")
    place = lax.axis_index("dp")
    core, quarter = place % 2, place // 2 % 4
    slabs = count // GROUP
    tokens, width = mixer.shape
    rows = width // count
    left = mixer.T.astype(jnp.float32).reshape(slabs, 4, 2, rows, tokens)
    mine = pick(left, core, 2)
    left = jnp.concatenate([mine, flip(pick(left, 1 - core, 2), 1)], axis=-1)
    lefts = []
    for offset in range(4):
        piece = pick(left, quarter ^ offset, 1).reshape(slabs * rows, 2 * tokens)
        lefts.append(flip(piece, 2 * offset) if offset else piece)
    right = upstream.astype(jnp.float32)
    right = jnp.concatenate([right, flip(right, 1)])
    right_y = flip(right, 4)
    rights = (right, flip(right, 2), right_y, flip(right_y, 2))
    product = factor_product(lefts, rights)
    return line_scatter(product.reshape(slabs, rows, right.shape[1]))


def local(
    tokens,
    cotangent,
    lengths,
    norm_gain,
    in_weight,
    conv_weight,
    conv_bias,
    dt_bias,
    a_log,
    skip_d,
    gate_gain,
    out_weight,
):
    count_rows = tokens.shape[0]
    segment_ids, live_rows = segment_rows(lengths, count_rows)
    float_rows = tokens.astype(jnp.float32)
    normed = norm_rows(float_rows, norm_gain).astype(jnp.bfloat16)
    projected = jnp.dot(normed, in_weight, preferred_element_type=jnp.float32)
    small_params = (conv_weight, conv_bias, dt_bias, a_log, skip_d, gate_gain)

    def local_mixer(proj_rows, params):
        return mixer_branch(
            proj_rows, segment_ids, params[0], params[1], params[2], params[3], params[4], params[5]
        )

    mixer_out, mixer_back = jax.vjp(local_mixer, projected, small_params)
    mixer_bf = mixer_out.astype(jnp.bfloat16)
    branch = jnp.dot(mixer_bf, out_weight, preferred_element_type=jnp.float32)
    output_rows = (float_rows + branch) * live_rows[:, None]
    upstream = cotangent * live_rows[:, None].astype(jnp.bfloat16)
    grad_mixer = lax.dot_general(
        upstream, out_weight, (((1,), (1,)), ((), ())), preferred_element_type=jnp.float32
    )
    grad_proj, grad_small = mixer_back(grad_mixer)
    grad_proj_bf = grad_proj.astype(jnp.bfloat16)
    grad_normed = lax.dot_general(
        grad_proj_bf, in_weight, (((1,), (1,)), ((), ())), preferred_element_type=jnp.float32
    )
    norm_value, norm_back = jax.vjp(norm_rows, float_rows, norm_gain)
    grad_rows, grad_gain = norm_back(grad_normed)
    grad_tokens = upstream.astype(jnp.float32) + grad_rows
    grad_in_share = sum_in_weight(normed, grad_proj_bf)
    grad_out_share = sum_out_weight(mixer_bf, upstream)
    small_sums = sum_all(
        (
            grad_gain,
            grad_small[0],
            grad_small[1],
            grad_small[2],
            grad_small[3],
            grad_small[4],
            grad_small[5],
        )
    )
    return (
        output_rows,
        grad_tokens,
        grad_in_share,
        grad_out_share,
        small_sums[0],
        small_sums[1],
        small_sums[2],
        small_sums[3],
        small_sums[4],
        small_sums[5],
        small_sums[6],
    )


def solution(mesh):
    return jax.shard_map(
        local,
        mesh=mesh,
        in_specs=(
            P("dp", None),
            P("dp", None),
            P("dp"),
            P(),
            P(),
            P(),
            P(),
            P(),
            P(),
            P(),
            P(),
            P(),
        ),
        out_specs=(
            P("dp", None),
            P("dp", None),
            P("dp", None),
            P("dp", None),
            P(),
            P(),
            P(),
            P(),
            P(),
            P(),
            P(),
        ),
        check_vma=False,
    )
```

```python
import functools
import math

import jax
import jax.numpy as jnp
from jax import lax
from jax.experimental import pallas as pl
from jax.experimental.pallas import tpu as pltpu
from jax.sharding import PartitionSpec as P

epsilon = 1e-05
highest = lax.Precision.HIGHEST
GROUP = 8
LANES = 128
BLOCK = 384
F32 = jnp.float32
BF16 = jnp.bfloat16


def flip(array, bits):
    count = lax.axis_size("dp")
    return lax.ppermute(array, "dp", [(i, i ^ bits) for i in range(count)])


def pick(array, index, axis=0):
    return lax.dynamic_index_in_dim(array, index, axis, keepdims=False)


def sum_all(flat):
    bits = 1
    while bits < lax.axis_size("dp"):
        flat = flat + flip(flat, bits)
        bits *= 2
    return flat


def line_scatter(parts):
    slabs = parts.shape[0]
    count = lax.axis_size("dp")
    slab = lax.axis_index("dp") // GROUP
    up_carry, down_carry = parts[slabs - 1], parts[0]
    for step in range(1, slabs):
        up_pairs = [(i, i + GROUP) for i in range(count - GROUP) if i // GROUP < step]
        down_pairs = [
            (i, i - GROUP) for i in range(GROUP, count) if slabs - 1 - i // GROUP < step
        ]
        up = lax.ppermute(up_carry, "dp", up_pairs)
        down = lax.ppermute(down_carry, "dp", down_pairs)
        if step < slabs - 1:
            up_carry = up + pick(parts, jnp.minimum(slabs - step + slab - 1, slabs - 1))
            down_carry = down + pick(parts, jnp.maximum(step - slabs + slab + 1, 0))
    return pick(parts, slab) + up + down


def product_kernel(lefts, rights, *refs):
    left_refs, right_refs = refs[:lefts], refs[lefts : lefts + rights]
    out_ref, right_held = refs[lefts + rights :]

    @pl.when(pl.program_id(0) == 0)
    def _():
        start = 0
        for ref in right_refs:
            right_held[start : start + ref.shape[0], :] = ref[...].astype(BF16)
            start += ref.shape[0]

    left = jnp.concatenate([ref[...].astype(BF16) for ref in left_refs], axis=1)
    out_ref[...] = jnp.dot(left, right_held[...], preferred_element_type=F32)


def factor_product(lefts, rights, block=128):
    rows = lefts[0].shape[0]
    depth = sum(left.shape[1] for left in lefts)
    columns = rights[0].shape[1]
    return pl.pallas_call(
        functools.partial(product_kernel, len(lefts), len(rights)),
        out_shape=jax.ShapeDtypeStruct((rows, columns), F32),
        grid=(rows // block,),
        in_specs=[pl.BlockSpec((block, left.shape[1]), lambda i: (i, 0)) for left in lefts]
        + [pl.BlockSpec(right.shape, lambda i: (0, 0)) for right in rights],
        out_specs=pl.BlockSpec((block, columns), lambda i: (i, 0)),
        scratch_shapes=[pltpu.VMEM((depth, columns), BF16)],
        cost_estimate=pl.CostEstimate(
            flops=2 * rows * depth * columns,
            bytes_accessed=4 * (rows * depth + depth * columns + rows * columns),
            transcendentals=0,
        ),
        name="factor_product",
    )(*lefts, *rights)


def segments(lengths_ref, shape, axis, delay=0):
    row = lax.broadcasted_iota(jnp.int32, shape, axis) - delay
    ids = jnp.zeros(shape, jnp.int32)
    end = jnp.int32(0)
    for slot in range(lengths_ref.shape[0]):
        end = end + lengths_ref[slot]
        ids = ids + (row >= end).astype(jnp.int32)
    return ids


def silu_parts(value):
    gate = jax.nn.sigmoid(value)
    return value * gate, gate * (1.0 + value * (1.0 - gate))


def project_kernel(lengths, x_ref, cot_ref, gain_ref, w_ref, proj_ref, left_ref, up_ref, held):
    @pl.when(pl.program_id(0) == 0)
    def _():
        x = x_ref[...].astype(F32)
        scale = lax.rsqrt(jnp.mean(x * x, axis=-1, keepdims=True) + epsilon)
        normed = (x * scale * gain_ref[...]).astype(BF16)
        held[...] = normed
        left_ref[...] = normed.astype(F32).T
        ids = segments(lengths, (x.shape[0], 1), 0)
        live = (ids < lengths.shape[0]).astype(F32)
        up_ref[...] = cot_ref[...].astype(F32) * live

    proj_ref[...] = jnp.dot(held[...], w_ref[...], preferred_element_type=F32)


def project(lengths, tokens, cotangent, gain, weight):
    rows, width = tokens.shape
    columns = -(-weight.shape[1] // BLOCK) * BLOCK
    whole = pl.BlockSpec((rows, width), lambda i: (0, 0))
    return pl.pallas_call(
        project_kernel,
        out_shape=(
            jax.ShapeDtypeStruct((rows, columns), F32),
            jax.ShapeDtypeStruct((width, rows), F32),
            jax.ShapeDtypeStruct((rows, width), F32),
        ),
        grid=(columns // BLOCK,),
        in_specs=[
            pl.BlockSpec(memory_space=pltpu.SMEM),
            whole,
            whole,
            pl.BlockSpec((1, width), lambda i: (0, 0)),
            pl.BlockSpec((width, BLOCK), lambda i: (0, i)),
        ],
        out_specs=(
            pl.BlockSpec((rows, BLOCK), lambda i: (0, i)),
            pl.BlockSpec((width, rows), lambda i: (0, 0)),
            whole,
        ),
        scratch_shapes=[pltpu.VMEM((rows, width), BF16)],
        cost_estimate=pl.CostEstimate(
            flops=2 * rows * width * columns,
            bytes_accessed=2 * width * columns + 4 * rows * columns,
            transcendentals=0,
        ),
        name="project",
    )(lengths, tokens, cotangent, gain, weight)


def conv_sum(u, taps, bias, masks):
    delayed = [u] + [pltpu.roll(u, d, 0) * masks[d - 1] for d in (1, 2, 3)]
    total = bias
    for d in range(4):
        total = total + taps[3 - d : 4 - d] * delayed[d]
    return total, delayed


def prepare(lengths, b_u, c_u, raw, b_taps, c_taps, b_bias, c_bias, dt_bias, a_log, heads, refs):
    masks, b_map, c_map, pairs, steps, logs, logs_t, transposed = refs
    rows = raw.shape[0]
    ids = segments(lengths, (rows, LANES), 0)
    time = lax.broadcasted_iota(jnp.int32, (rows, LANES), 0)
    for d in (1, 2, 3):
        same = (segments(lengths, (rows, LANES), 0, d) == ids) & (time >= d)
        masks[d - 1] = same.astype(F32)
    taken = [masks[d] for d in range(3)]
    b_sum, _ = conv_sum(b_u, b_taps, b_bias, taken)
    c_sum, _ = conv_sum(c_u, c_taps, c_bias, taken)
    b_value = b_sum * jax.nn.sigmoid(b_sum)
    c_value = c_sum * jax.nn.sigmoid(c_sum)
    b_map[...], c_map[...] = b_value, c_value
    first = lax.broadcasted_iota(jnp.int32, (rows, rows), 0)
    second = lax.broadcasted_iota(jnp.int32, (rows, rows), 1)
    same = segments(lengths, (rows, rows), 0) == segments(lengths, (rows, rows), 1)
    contract = (((1,), (1,)), ((), ()))
    if transposed:
        inner = lax.dot_general(b_value, c_value, contract, precision=highest)
        pairs[...] = jnp.where(same & (first <= second), inner, 0.0)
    else:
        inner = lax.dot_general(c_value, b_value, contract, precision=highest)
        pairs[...] = jnp.where(same & (first >= second), inner, 0.0)
    lane = lax.broadcasted_iota(jnp.int32, (rows, LANES), 1)
    total = raw + dt_bias
    step = jnp.maximum(total, 0.0) + jnp.log1p(jnp.exp(-jnp.abs(total)))
    step = jnp.where(lane < heads, step, 0.0)
    steps[...] = step
    log = step * (jnp.exp(a_log) * -math.log2(math.e))
    lower = (first >= second).astype(F32)
    sums = jnp.dot(lower, log, precision=highest, preferred_element_type=F32)
    logs[...] = sums
    logs_t[...] = sums.T


def column(array, lane, index):
    return jnp.sum(jnp.where(lane == index, array, 0.0), axis=1, keepdims=True)


def forward_kernel(
    heads,
    lengths,
    gate_ref,
    u_ref,
    b_ref,
    c_ref,
    raw_ref,
    taps_ref,
    b_taps_ref,
    c_taps_ref,
    bias_ref,
    b_bias_ref,
    c_bias_ref,
    dt_ref,
    a_ref,
    skip_ref,
    gain_ref,
    mixed_ref,
    mixer_ref,
    left_ref,
    scale_ref,
    masks,
    b_map,
    c_map,
    pairs,
    steps,
    logs,
    logs_t,
    gated_held,
    squares,
):
    tile = pl.program_id(0)
    tiles = pl.num_programs(0)
    rows = u_ref.shape[0]

    @pl.when(tile == 0)
    def _():
        prepare(
            lengths,
            b_ref[...],
            c_ref[...],
            raw_ref[...],
            b_taps_ref[...],
            c_taps_ref[...],
            b_bias_ref[...],
            c_bias_ref[...],
            dt_ref[...],
            a_ref[...],
            heads,
            (masks, b_map, c_map, pairs, steps, logs, logs_t, False),
        )
        squares[...] = jnp.zeros_like(squares)

    lane = lax.broadcasted_iota(jnp.int32, (rows, LANES), 1)
    low = lane < LANES // 2
    total, _ = conv_sum(u_ref[...], taps_ref[...], bias_ref[...], [masks[d] for d in range(3)])
    values = total * jax.nn.sigmoid(total)
    step = steps[...]
    step = jnp.where(low, column(step, lane, 2 * tile), column(step, lane, 2 * tile + 1))
    scaled = (values * step).astype(BF16)
    halves = []
    for half in range(2):
        head = 2 * tile + half
        log_t = column(logs[...], lane, head)
        log_s = logs_t[pl.ds(head, 1), :]
        parts = []
        for start in range(0, rows, LANES):
            stop = start + LANES
            decay = jnp.exp2(jnp.minimum(log_t[start:stop] - log_s[:, :stop], 0.0))
            mixing = (decay * pairs[start:stop, :stop]).astype(BF16)
            parts.append(jnp.dot(mixing, scaled[:stop], preferred_element_type=F32))
        halves.append(jnp.concatenate(parts, axis=0))
    mixed = jnp.where(low, halves[0], halves[1]) + skip_ref[...] * values
    mixed_ref[...] = mixed
    gate = gate_ref[...]
    gated = mixed * (gate * jax.nn.sigmoid(gate))
    gated_held[tile] = gated
    squares[...] += gated * gated

    @pl.when(tile == tiles - 1)
    def _():
        mean = jnp.sum(squares[...], axis=1, keepdims=True) / (tiles * LANES)
        scale = lax.rsqrt(mean + epsilon)
        scale_ref[...] = jnp.broadcast_to(scale, scale_ref.shape)

        def finish(index, _):
            here = pl.ds(pl.multiple_of(index * LANES, LANES), LANES)
            normed = (gated_held[index] * scale * gain_ref[:, here]).astype(BF16)
            mixer_ref[:, here] = normed
            left_ref[here, :] = normed.astype(F32).T
            return 0

        lax.fori_loop(0, gated_held.shape[0], finish, 0)


def scan_specs(rows, tiles, of_tile):
    fixed = lambda index: pl.BlockSpec((rows, LANES), lambda i: (0, index))
    taps = lambda index: pl.BlockSpec((4, LANES), lambda i: (0, index))
    bias = lambda index: pl.BlockSpec((1, LANES), lambda i: (0, index))
    return [
        pl.BlockSpec((rows, LANES), lambda i: (0, tiles + of_tile(i))),
        fixed(2 * tiles),
        fixed(2 * tiles + 1),
        fixed(2 * tiles + 2),
        pl.BlockSpec((4, LANES), lambda i: (0, of_tile(i))),
        taps(tiles),
        taps(tiles + 1),
        pl.BlockSpec((1, LANES), lambda i: (0, of_tile(i))),
        bias(tiles),
        bias(tiles + 1),
        bias(0),
        bias(0),
    ]


def scan_scratch(rows):
    return [
        pltpu.VMEM((3, rows, LANES), F32),
        pltpu.VMEM((rows, LANES), F32),
        pltpu.VMEM((rows, LANES), F32),
        pltpu.VMEM((rows, rows), F32),
        pltpu.VMEM((rows, LANES), F32),
        pltpu.VMEM((rows, LANES), F32),
        pltpu.VMEM((LANES, rows), F32),
    ]


def mixer_forward(lengths, proj, conv_weight, conv_bias, dt_bias, a_log, skip, gain, heads):
    rows = proj.shape[0]
    inner = gain.shape[1]
    tiles = inner // LANES
    own = lambda i: (0, i)
    specs = scan_specs(rows, tiles, lambda i: i)
    return pl.pallas_call(
        functools.partial(forward_kernel, heads),
        out_shape=(
            jax.ShapeDtypeStruct((rows, inner), F32),
            jax.ShapeDtypeStruct((rows, inner), BF16),
            jax.ShapeDtypeStruct((inner, rows), F32),
            jax.ShapeDtypeStruct((rows, LANES), F32),
        ),
        grid=(tiles,),
        in_specs=[pl.BlockSpec(memory_space=pltpu.SMEM), pl.BlockSpec((rows, LANES), own)]
        + specs
        + [pl.BlockSpec((1, LANES), own), pl.BlockSpec((1, inner), lambda i: (0, 0))],
        out_specs=(
            pl.BlockSpec((rows, LANES), own),
            pl.BlockSpec((rows, inner), lambda i: (0, 0)),
            pl.BlockSpec((inner, rows), lambda i: (0, 0)),
            pl.BlockSpec((rows, LANES), lambda i: (0, 0)),
        ),
        scratch_shapes=scan_scratch(rows)
        + [pltpu.VMEM((tiles, rows, LANES), F32), pltpu.VMEM((rows, LANES), F32)],
        cost_estimate=pl.CostEstimate(
            flops=2 * heads * rows * rows * LANES,
            bytes_accessed=4 * 5 * rows * inner,
            transcendentals=heads * rows * rows,
        ),
        name="mixer_forward",
    )(
        lengths,
        proj,
        proj,
        proj,
        proj,
        proj,
        conv_weight,
        conv_weight,
        conv_weight,
        conv_bias,
        conv_bias,
        conv_bias,
        dt_bias,
        a_log,
        skip,
        gain,
    )


def gate_kernel(
    up_ref,
    weight_ref,
    mixed_ref,
    gate_ref,
    scale_ref,
    gain_ref,
    grad_mixed_ref,
    grad_gate_ref,
    quarters_ref,
    grad_gain_ref,
    up_held,
    mixed_held,
    gate_held,
    grad_held,
    dots,
):
    index = pl.program_id(0)
    blocks = pl.num_programs(0)

    @pl.when(index == 0)
    def _():
        up_held[...] = up_ref[...].astype(BF16)
        dots[...] = jnp.zeros_like(dots)

    grad = lax.dot_general(
        up_held[...], weight_ref[...], (((1,), (1,)), ((), ())), preferred_element_type=F32
    )
    gate = gate_ref[...]
    mixed = mixed_ref[...]
    gated = mixed * (gate * jax.nn.sigmoid(gate))
    here = pl.ds(pl.multiple_of(index * BLOCK, BLOCK), BLOCK)
    terms = grad * gain_ref[:, here] * gated
    for start in range(0, BLOCK, LANES):
        dots[...] += terms[:, start : start + LANES]
    grad_held[index] = grad
    mixed_held[index] = mixed
    gate_held[index] = gate

    @pl.when(index == blocks - 1)
    def _():
        scale = scale_ref[...][:, :1]
        shared = jnp.sum(dots[...], axis=1, keepdims=True) * scale * scale / (blocks * BLOCK)

        def finish(step, _):
            here = pl.ds(pl.multiple_of(step * BLOCK, BLOCK), BLOCK)
            grad = grad_held[step]
            mixed = mixed_held[step]
            passed, slope = silu_parts(gate_held[step])
            gated = mixed * passed
            grad_gain_ref[:, here] = jnp.sum(grad * gated * scale, axis=0, keepdims=True)
            back = scale * (grad * gain_ref[:, here] - gated * shared)
            grad_mixed_ref[:, here] = back * passed
            rounded = (back * mixed * slope).astype(BF16)
            grad_gate_ref[:, here] = rounded
            widened = rounded.astype(F32)
            half = pl.multiple_of((step % 2) * BLOCK, BLOCK)
            quarters_ref[step // 2, :, pl.ds(half, BLOCK)] = widened
            return 0

        lax.fori_loop(0, grad_held.shape[0], finish, 0)


def gate_backward(upstream, weight, mixed, proj, scale, gain):
    rows, width = upstream.shape
    inner = gain.shape[1]
    blocks = inner // BLOCK
    own = pl.BlockSpec((rows, BLOCK), lambda i: (0, i))
    held = pltpu.VMEM((blocks, rows, BLOCK), F32)
    return pl.pallas_call(
        gate_kernel,
        out_shape=(
            jax.ShapeDtypeStruct((rows, inner), F32),
            jax.ShapeDtypeStruct((rows, inner), BF16),
            jax.ShapeDtypeStruct((4, rows, inner // 4), F32),
            jax.ShapeDtypeStruct((1, inner), F32),
        ),
        grid=(blocks,),
        in_specs=[
            pl.BlockSpec((rows, width), lambda i: (0, 0)),
            pl.BlockSpec((BLOCK, width), lambda i: (i, 0)),
            own,
            own,
            pl.BlockSpec((rows, LANES), lambda i: (0, 0)),
            pl.BlockSpec((1, inner), lambda i: (0, 0)),
        ],
        out_specs=(
            pl.BlockSpec((rows, inner), lambda i: (0, 0)),
            pl.BlockSpec((rows, inner), lambda i: (0, 0)),
            pl.BlockSpec((4, rows, inner // 4), lambda i: (0, 0, 0)),
            pl.BlockSpec((1, inner), lambda i: (0, 0)),
        ),
        scratch_shapes=[
            pltpu.VMEM((rows, width), BF16),
            held,
            held,
            held,
            pltpu.VMEM((rows, LANES), F32),
        ],
        cost_estimate=pl.CostEstimate(
            flops=2 * rows * width * inner,
            bytes_accessed=2 * width * inner + 4 * 6 * rows * inner,
            transcendentals=rows * inner,
        ),
        name="gate_backward",
    )(upstream, weight, mixed, proj, scale, gain)


def state_kernel(
    heads,
    tiles,
    lengths,
    u_ref,
    b_ref,
    c_ref,
    raw_ref,
    taps_ref,
    b_taps_ref,
    c_taps_ref,
    bias_ref,
    b_bias_ref,
    c_bias_ref,
    dt_ref,
    a_ref,
    skip_ref,
    mixed_ref,
    grad_ref,
    rounded_ref,
    quarter_ref,
    small_ref,
    masks,
    b_map,
    c_map,
    pairs,
    steps,
    logs,
    logs_t,
    grad_pairs,
    grad_steps,
    changes,
    skip_sums,
):
    tile = pl.program_id(0)
    rows = u_ref.shape[0]
    lane = lax.broadcasted_iota(jnp.int32, (rows, LANES), 1)

    @pl.when(tile == 0)
    def _():
        prepare(
            lengths,
            b_ref[...],
            c_ref[...],
            raw_ref[...],
            b_taps_ref[...],
            c_taps_ref[...],
            b_bias_ref[...],
            c_bias_ref[...],
            dt_ref[...],
            a_ref[...],
            heads,
            (masks, b_map, c_map, pairs, steps, logs, logs_t, True),
        )
        for ref in (grad_pairs, grad_steps, changes, skip_sums):
            ref[...] = jnp.zeros_like(ref)

    def store(grad):
        rounded = grad.astype(BF16)
        rounded_ref[...] = rounded
        quarter_ref[0] = rounded.astype(F32)

    def conv_back(grad, u, taps, bias):
        taken = [masks[d] for d in range(3)]
        total, delayed = conv_sum(u, taps, bias, taken)
        _, slope = silu_parts(total)
        grad = grad * slope
        small_ref[4:5, :] = jnp.sum(grad, axis=0, keepdims=True)
        back = taps[3:4] * grad
        small_ref[3:4, :] = jnp.sum(grad * delayed[0], axis=0, keepdims=True)
        for d in (1, 2, 3):
            small_ref[3 - d : 4 - d, :] = jnp.sum(grad * delayed[d], axis=0, keepdims=True)
            back = back + taps[3 - d : 4 - d] * pltpu.roll(grad * taken[d - 1], rows - d, 0)
        store(back)

    @pl.when(tile < tiles)
    def _():
        low = lane < LANES // 2
        u, taps, bias = u_ref[...], taps_ref[...], bias_ref[...]
        total, _ = conv_sum(u, taps, bias, [masks[d] for d in range(3)])
        values = total * jax.nn.sigmoid(total)
        step = steps[...]
        step = jnp.where(low, column(step, lane, 2 * tile), column(step, lane, 2 * tile + 1))
        scaled = (values * step).astype(BF16)
        grad = grad_ref[...]
        grad_bf = grad.astype(BF16)
        skip = skip_ref[...]
        halves = []
        for half in range(2):
            head = 2 * tile + half
            ours = low if half == 0 else jnp.logical_not(low)
            mine = jnp.where(ours, scaled, jnp.zeros_like(scaled))
            log_s = column(logs[...], lane, head)
            log_t = logs_t[pl.ds(head, 1), :]
            parts = []
            for start in range(0, rows, LANES):
                stop = start + LANES
                decay = jnp.exp2(jnp.minimum(log_t[:, start:] - log_s[start:stop], 0.0))
                mixing = (decay * pairs[start:stop, start:]).astype(BF16)
                parts.append(jnp.dot(mixing, grad_bf[start:], preferred_element_type=F32))
                outer = lax.dot_general(
                    mine[start:stop],
                    grad_bf[start:],
                    (((1,), (1,)), ((), ())),
                    preferred_element_type=F32,
                )
                grad_pairs[start:stop, start:] += decay * outer
            halves.append(jnp.concatenate(parts, axis=0))
        back = jnp.where(low, halves[0], halves[1])
        from_lane = lax.broadcasted_iota(jnp.int32, (LANES, LANES), 0)
        to_lane = lax.broadcasted_iota(jnp.int32, (LANES, LANES), 1)
        own = 2 * tile + (from_lane >= LANES // 2).astype(jnp.int32)
        to_head = (to_lane == own).astype(F32)
        grad_steps[...] += jnp.dot(values * back, to_head, precision=highest)
        unskipped = mixed_ref[...] - skip * values
        moved = grad_bf.astype(F32) * unskipped - scaled.astype(F32) * back
        changes[...] += jnp.dot(moved, to_head, precision=highest)
        direct = (grad * values).reshape(rows // 8, 8, LANES).sum(axis=0)
        skip_sums[...] += jnp.dot(direct, to_head, precision=highest)
        small_ref[...] = jnp.zeros_like(small_ref)
        conv_back(back * step + skip * grad, u, taps, bias)

    first = lax.broadcasted_iota(jnp.int32, (rows, rows), 0)
    second = lax.broadcasted_iota(jnp.int32, (rows, rows), 1)

    @pl.when(tile == tiles)
    def _():
        same = segments(lengths, (rows, rows), 0) == segments(lengths, (rows, rows), 1)
        grad_pairs[...] = jnp.where(same & (first <= second), grad_pairs[...], 0.0)
        grad = jnp.dot(grad_pairs[...], c_map[...], precision=highest)
        small_ref[...] = jnp.zeros_like(small_ref)
        conv_back(grad, b_ref[...], b_taps_ref[...], b_bias_ref[...])

    @pl.when(tile == tiles + 1)
    def _():
        grad = lax.dot_general(
            grad_pairs[...], b_map[...], (((0,), (0,)), ((), ())), precision=highest
        )
        small_ref[...] = jnp.zeros_like(small_ref)
        conv_back(grad, c_ref[...], c_taps_ref[...], c_bias_ref[...])

    @pl.when(tile == tiles + 2)
    def _():
        step = steps[...]
        direct = grad_steps[...]
        later = (second >= first).astype(F32)
        grad_log = jnp.dot(later, changes[...], precision=highest)
        rate = jnp.exp(a_ref[...])
        total = raw_ref[...] + dt_ref[...]
        grad = (direct - grad_log * rate) * jax.nn.sigmoid(total)
        grad = jnp.where(lane < heads, grad, 0.0)
        small_ref[...] = jnp.zeros_like(small_ref)
        small_ref[0:1, :] = jnp.sum(grad, axis=0, keepdims=True)
        small_ref[1:2, :] = jnp.sum(grad_log * step, axis=0, keepdims=True) * -rate
        small_ref[2:3, :] = jnp.sum(skip_sums[...], axis=0, keepdims=True)
        store(grad)

    @pl.when(tile > tiles + 2)
    def _():
        small_ref[...] = jnp.zeros_like(small_ref)
        store(jnp.zeros((rows, LANES), F32))


def state_backward(
    lengths, proj, conv_weight, conv_bias, dt_bias, a_log, skip, mixed, grad_mixed, heads
):
    rows, inner = mixed.shape
    tiles = inner // LANES
    padded = -(-(tiles + 3) // 4) * 4
    each = padded // 4
    of_tile = lambda i: jnp.minimum(i, tiles - 1)
    own = lambda i: (0, jnp.minimum(i, tiles - 1))
    specs = scan_specs(rows, tiles, of_tile)
    return pl.pallas_call(
        functools.partial(state_kernel, heads, tiles),
        out_shape=(
            jax.ShapeDtypeStruct((rows, padded * LANES), BF16),
            jax.ShapeDtypeStruct((4, rows, each * LANES), F32),
            jax.ShapeDtypeStruct((8, padded * LANES), F32),
        ),
        grid=(padded,),
        in_specs=[pl.BlockSpec(memory_space=pltpu.SMEM)]
        + specs
        + [
            pl.BlockSpec((1, LANES), own),
            pl.BlockSpec((rows, LANES), own),
            pl.BlockSpec((rows, LANES), own),
        ],
        out_specs=(
            pl.BlockSpec((rows, LANES), lambda i: (0, i)),
            pl.BlockSpec((1, rows, LANES), lambda i: (i // each, 0, i % each)),
            pl.BlockSpec((8, LANES), lambda i: (0, i)),
        ),
        scratch_shapes=scan_scratch(rows)
        + [
            pltpu.VMEM((rows, rows), F32),
            pltpu.VMEM((rows, LANES), F32),
            pltpu.VMEM((rows, LANES), F32),
            pltpu.VMEM((8, LANES), F32),
        ],
        cost_estimate=pl.CostEstimate(
            flops=4 * heads * rows * rows * LANES,
            bytes_accessed=4 * 5 * rows * inner,
            transcendentals=heads * rows * rows,
        ),
        name="state_backward",
    )(
        lengths,
        proj,
        proj,
        proj,
        proj,
        conv_weight,
        conv_weight,
        conv_weight,
        conv_bias,
        conv_bias,
        conv_bias,
        dt_bias,
        a_log,
        skip,
        mixed,
        grad_mixed,
    )


def output_kernel(lengths, mixer_ref, weight_ref, x_ref, out_ref):
    branch = jnp.dot(mixer_ref[...], weight_ref[...], preferred_element_type=F32)
    ids = segments(lengths, (x_ref.shape[0], 1), 0)
    live = (ids < lengths.shape[0]).astype(F32)
    out_ref[...] = (x_ref[...].astype(F32) + branch) * live


def block_output(lengths, mixer, weight, tokens):
    rows, width = tokens.shape
    inner = mixer.shape[1]
    own = pl.BlockSpec((rows, 256), lambda i: (0, i))
    return pl.pallas_call(
        output_kernel,
        out_shape=jax.ShapeDtypeStruct((rows, width), F32),
        grid=(width // 256,),
        in_specs=[
            pl.BlockSpec(memory_space=pltpu.SMEM),
            pl.BlockSpec((rows, inner), lambda i: (0, 0)),
            pl.BlockSpec((inner, 256), lambda i: (0, i)),
            own,
        ],
        out_specs=own,
        cost_estimate=pl.CostEstimate(
            flops=2 * rows * width * inner,
            bytes_accessed=2 * width * inner + 6 * rows * width,
            transcendentals=0,
        ),
        name="block_output",
    )(lengths, mixer, weight, tokens)


def token_kernel(
    columns, split, gate_ref, conv_ref, weight_ref, x_ref, gain_ref, up_ref, out_ref, sums_ref, held
):
    index = pl.program_id(0)
    blocks = pl.num_programs(0)
    contract = (((1,), (1,)), ((), ()))

    @pl.when(index == 0)
    def _():
        held[...] = jnp.zeros_like(held)

    @pl.when(index < split)
    def _():
        held[...] += lax.dot_general(
            gate_ref[...], weight_ref[...], contract, preferred_element_type=F32
        )

    @pl.when((index >= split) & (index < blocks - 1))
    def _():
        held[...] += lax.dot_general(
            conv_ref[...], weight_ref[...], contract, preferred_element_type=F32
        )

    @pl.when(index == blocks - 1)
    def _():
        weight = weight_ref[...]
        lane = lax.broadcasted_iota(jnp.int32, weight.shape, 1)
        weight = jnp.where(lane < columns - (blocks - 1) * BLOCK, weight, jnp.zeros_like(weight))
        grad = held[...] + lax.dot_general(
            conv_ref[...], weight, contract, preferred_element_type=F32
        )
        x = x_ref[...].astype(F32)
        scale = lax.rsqrt(jnp.mean(x * x, axis=-1, keepdims=True) + epsilon)
        unit = x * scale
        sums_ref[...] = jnp.sum(grad * unit, axis=0, keepdims=True)
        grad = grad * gain_ref[...]
        shared = jnp.mean(grad * unit, axis=-1, keepdims=True)
        out_ref[...] = up_ref[...] + scale * (grad - unit * shared)


def token_backward(grad_gate, grad_conv, weight, tokens, gain, upstream):
    rows, width = tokens.shape
    columns = weight.shape[1]
    blocks = -(-columns // BLOCK)
    split = grad_gate.shape[1] // BLOCK
    whole = pl.BlockSpec((rows, width), lambda i: (0, 0))
    line = pl.BlockSpec((1, width), lambda i: (0, 0))
    return pl.pallas_call(
        functools.partial(token_kernel, columns, split),
        out_shape=(
            jax.ShapeDtypeStruct((rows, width), F32),
            jax.ShapeDtypeStruct((1, width), F32),
        ),
        grid=(blocks,),
        in_specs=[
            pl.BlockSpec((rows, BLOCK), lambda i: (0, jnp.minimum(i, split - 1))),
            pl.BlockSpec((rows, BLOCK), lambda i: (0, jnp.maximum(i - split, 0))),
            pl.BlockSpec((width, BLOCK), lambda i: (0, i)),
            whole,
            line,
            whole,
        ],
        out_specs=(whole, line),
        scratch_shapes=[pltpu.VMEM((rows, width), F32)],
        cost_estimate=pl.CostEstimate(
            flops=2 * rows * width * columns,
            bytes_accessed=2 * width * columns + 10 * rows * width,
            transcendentals=0,
        ),
        name="token_backward",
    )(grad_gate, grad_conv, weight, tokens, gain, upstream)


def arrange_kernel(gate, quarter_ref, first, second, third, fourth, out_ref, held):
    quarter = quarter_ref[0]

    conv = first.shape[1] - gate
    for offset, ref in enumerate((first, second, third, fourth)):
        source = lax.bitwise_xor(quarter, offset)
        held[:, pl.ds(pl.multiple_of(source * gate, LANES), gate)] = ref[:, :gate]
        start = pl.multiple_of(4 * gate + source * conv, LANES)
        held[:, pl.ds(start, conv)] = ref[:, gate:]
    out_ref[...] = held[:, : out_ref.shape[1]]


def arrange(quarter, pieces, gate, columns):
    rows, each = pieces[0].shape
    return pl.pallas_call(
        functools.partial(arrange_kernel, gate),
        out_shape=jax.ShapeDtypeStruct((rows, columns), F32),
        in_specs=[pl.BlockSpec(memory_space=pltpu.SMEM)]
        + [pl.BlockSpec(memory_space=pltpu.VMEM)] * 4,
        out_specs=pl.BlockSpec(memory_space=pltpu.VMEM),
        scratch_shapes=[pltpu.VMEM((rows, 4 * each), F32)],
        name="arrange",
    )(quarter.reshape(1), *pieces)


def local(
    tokens,
    cotangent,
    lengths,
    norm_gain,
    in_weight,
    conv_weight,
    conv_bias,
    dt_bias,
    a_log,
    skip_d,
    gate_gain,
    out_weight,
):
    count = lax.axis_size("dp")
    place = lax.axis_index("dp")
    core, quarter = place % 2, place // 2 % 4
    slabs = count // GROUP
    rows, width = tokens.shape
    inner, heads = gate_gain.shape[0], a_log.shape[0]
    in_rows, out_rows = width // count, inner // count
    columns = in_weight.shape[1]
    norm_line = norm_gain.reshape(1, -1)
    gain_line = gate_gain.reshape(1, -1)
    bias_line = conv_bias.reshape(1, -1)
    dt_line = jnp.pad(dt_bias, (0, LANES - heads)).reshape(1, -1)
    a_line = jnp.pad(a_log, (0, LANES - heads)).reshape(1, -1)
    skip_line = jnp.repeat(skip_d, inner // heads).reshape(1, -1)

    proj, left_in, upstream = project(lengths, tokens, cotangent, norm_line, in_weight)

    left_in = left_in.reshape(slabs * 4, 2, in_rows, rows)
    own = pick(left_in, core, 1)
    left_in = jnp.concatenate([own, flip(pick(left_in, 1 - core, 1), 1)], axis=-1)
    left_in = left_in.reshape(width // 2, 2 * rows)
    left_in_x = flip(left_in, 2)
    lefts_in = (left_in, left_in_x, flip(left_in, 4), flip(left_in_x, 4))

    mixed, mixer, left_out, scale = mixer_forward(
        lengths, proj, conv_weight, bias_line, dt_line, a_line, skip_line, gain_line, heads
    )
    grad_mixed, grad_gate, gate_parts, gain_sums = gate_backward(
        upstream, out_weight, mixed, proj, scale, gain_line
    )
    gate_rights = []
    for offset in range(4):
        piece = pick(gate_parts, quarter ^ offset)
        if offset:
            piece = flip(piece, 2 * offset)
        gate_rights += [piece, flip(piece, 1)]

    grad_conv, conv_parts, small = state_backward(
        lengths, proj, conv_weight, bias_line, dt_line, a_line, skip_line, mixed, grad_mixed, heads
    )
    conv_rights = []
    for offset in range(4):
        piece = pick(conv_parts, quarter ^ offset)
        if offset:
            piece = flip(piece, 2 * offset)
        conv_rights += [piece, flip(piece, 1)]

    rights_out = jnp.concatenate([upstream, flip(upstream, 1)])
    rights_out_y = flip(rights_out, 4)
    rights_out = (rights_out, flip(rights_out, 2), rights_out_y, flip(rights_out_y, 2))

    left_out = left_out.reshape(slabs, 4, 2, out_rows, rows)
    own = pick(left_out, core, 2)
    left_out = jnp.concatenate([own, flip(pick(left_out, 1 - core, 2), 1)], axis=-1)
    lefts_out = []
    for offset in range(4):
        piece = pick(left_out, quarter ^ offset, 1).reshape(slabs * out_rows, 2 * rows)
        lefts_out.append(flip(piece, 2 * offset) if offset else piece)

    output_rows = block_output(lengths, mixer, out_weight, tokens)
    grad_tokens, norm_sums = token_backward(
        grad_gate, grad_conv, in_weight, tokens, norm_line, upstream
    )

    flat = jnp.concatenate([small.reshape(-1), gain_sums.reshape(-1), norm_sums.reshape(-1)])
    flat = sum_all(flat)
    taken = small.size
    small = flat[:taken].reshape(small.shape)
    gain_sums = flat[taken : taken + inner]
    norm_sums = flat[taken + inner :]
    channels = conv_bias.shape[0]
    heads_at = channels

    gate_share = line_scatter(
        factor_product(lefts_in, gate_rights).reshape(slabs, 4, in_rows, inner // 4)
    )
    conv_share = line_scatter(
        factor_product(lefts_in, conv_rights).reshape(slabs, 4, in_rows, -1)
    )
    share = jnp.concatenate([gate_share, conv_share], axis=-1)
    pieces = [pick(share, quarter)]
    pieces += [flip(pick(share, quarter ^ offset), 2 * offset) for offset in (1, 2, 3)]
    grad_in = arrange(quarter, pieces, inner // 4, columns)
    grad_out = line_scatter(
        factor_product(lefts_out, rights_out).reshape(slabs, out_rows, width)
    )
    return (
        output_rows,
        grad_tokens,
        grad_in,
        grad_out,
        norm_sums,
        small[:4, :channels],
        small[4, :channels],
        small[0, heads_at : heads_at + heads],
        small[1, heads_at : heads_at + heads],
        small[2, heads_at : heads_at + heads],
        gain_sums,
    )


def solution(mesh):
    return jax.shard_map(
        local,
        mesh=mesh,
        in_specs=(
            P("dp", None),
            P("dp", None),
            P("dp"),
            P(),
            P(),
            P(),
            P(),
            P(),
            P(),
            P(),
            P(),
            P(),
        ),
        out_specs=(
            P("dp", None),
            P("dp", None),
            P("dp", None),
            P("dp", None),
            P(),
            P(),
            P(),
            P(),
            P(),
            P(),
            P(),
        ),
        check_vma=False,
    )
```
